32 devices in a mesh: parts: 2 (over y), panel: 4 (over z), zone: 2 (over x), rhs: 2 (over core).
Axes of the slice: x: 2, y: 2, z: 4, core: 2. Of those that a mesh axis runs over, the one named last changes fastest.
Arguments:
- source: bfloat16 [4, 4096, 512], P(('parts', 'zone'), 'panel', 'rhs'), parts along dimension 0, may hold values from -6 to 6
- inverse: bfloat16 [4, 4096, 4096], P(('parts', 'zone'), 'panel'), parts along dimension 0, may hold values from -0.09375 to 0.09375
- coupling: bfloat16 [4, 4096, 4096], P(('parts', 'zone'), 'panel'), parts along dimension 0, may hold values from -0.078125 to 0.078125
Outputs:
- eliminated: bfloat16 [4, 4096, 512], P(('parts', 'zone'), 'panel', 'rhs'), parts along dimension 0
The draws below stay inside these ranges and needn't reach their ends.
There are 2 independent parts, one for each index of `parts`. The reference program is written for one: setup_inputs(seed, part) draws one part's arguments, and reference() takes and returns one part's arrays. A program takes and returns all parts, laid end to end along the dimension named above; each array names one. Nothing has to cross between parts.
All inputs are finite; a program needn't handle non-finite values.
Results may differ from the reference program's by a relative error of at most 0.013.
Values may be sent and summed in bfloat16 or wider, within the bound.
No kernel may reach another device: no remote copies, remote signals or barrier semaphores. Data moves between devices by JAX's collectives and lax.ppermute only.
A program may use at most 64 MiB of HBM per device.

```python
import jax
import jax.numpy as jnp
from jax import lax

BLOCK = 4096
RHS = 512
ZONES = 2


def level_of(key, shape, cuts, least, top_value):
    factor_of = 1.0
    for dim, shards_of in cuts:
        heights = jax.random.uniform(jax.random.fold_in(jax.random.fold_in(key, 6), dim), (shards_of,), jnp.float32, least / len(cuts), top_value / len(cuts))
        factor_of = factor_of * jnp.repeat(jnp.exp(heights), shape[dim] // shards_of).reshape((-1,) + (1,) * (len(shape) - 1 - dim))
    return factor_of


def centred(stream_key, dims, scale, bound, shards=(), held_as=jnp.bfloat16):
    entries = jax.random.normal(stream_key, dims, jnp.float32) * scale
    if len(shards) > 0:
        entries = level_of(stream_key, dims, shards, -0.22, 0.18) * entries
    return jnp.clip(entries, min=-bound, max=bound).astype(held_as)


def setup_inputs(seed: int = 0, part: int = 0) -> dict:
    key_list = jax.random.split(jax.random.key(seed), 4)
    own_keys = jax.random.split(jax.random.fold_in(key_list[3], part), 4)
    return {
        "source": centred(own_keys[0], (ZONES, BLOCK, RHS), 1.0, 6.0, ((0, 2), (1, 4), (2, 2))),
        "inverse": centred(own_keys[1], (ZONES, BLOCK, BLOCK), BLOCK ** -0.5, 0.09375, ((0, 2), (1, 4))),
        "coupling": centred(own_keys[2], (ZONES, BLOCK, BLOCK), (BLOCK * 5 // 4) ** -0.5, 0.078125, ((0, 2), (1, 4))),
    }


def reference(source, inverse, coupling):
    def eliminate(previous, inputs):
        source_zone, inverse_zone, coupling_zone = inputs
        projected = jnp.dot(inverse_zone, source_zone, preferred_element_type=jnp.float32)
        combined = projected - jnp.dot(coupling_zone, previous, preferred_element_type=jnp.float32)
        rounded = combined.astype(jnp.bfloat16)
        return rounded, rounded

    initial = jnp.zeros((BLOCK, RHS), jnp.bfloat16)
    _, result = lax.scan(eliminate, initial, (source, inverse, coupling))
    return result
```

```python
import functools

import jax
import jax.numpy as jnp
from jax import lax
from jax.experimental import pallas as pl
from jax.experimental.pallas import tpu as pltpu
from jax.sharding import PartitionSpec as P

CHUNKS = 2
MIB = 1 << 20
VMEM = pl.BlockSpec(memory_space=pltpu.VMEM)
HBM = pl.BlockSpec(memory_space=pltpu.HBM)


def params(mib):
    return pltpu.CompilerParams(vmem_limit_bytes=mib * MIB)


def fetch_kernel(first, second, first_out, second_out, sems):
    copies = [
        pltpu.make_async_copy(first, first_out, sems.at[0]),
        pltpu.make_async_copy(second, second_out, sems.at[1]),
    ]
    for copy in copies:
        copy.start()
    for copy in copies:
        copy.wait()


def fetch(inverse, coupling):
    shape = jax.ShapeDtypeStruct(inverse.shape, inverse.dtype)
    return pl.pallas_call(
        fetch_kernel,
        out_shape=(shape, shape),
        in_specs=[HBM, HBM],
        out_specs=(VMEM, VMEM),
        scratch_shapes=[pltpu.SemaphoreType.DMA((2,))],
        compiler_params=params(18),
        name="fetch",
    )(inverse, coupling)


def relay_kernel(own, up, down, out):
    me = lax.axis_index("panel")

    @pl.when(me == 2)
    def _():
        out[...] = up[...]

    @pl.when(me == 1)
    def _():
        out[...] = down[...]

    @pl.when(jnp.logical_and(me != 1, me != 2))
    def _():
        out[...] = own[...]


def relay(own, up, down):
    return pl.pallas_call(
        relay_kernel,
        out_shape=jax.ShapeDtypeStruct(own.shape, own.dtype),
        in_specs=[VMEM] * 3,
        out_specs=VMEM,
        compiler_params=params(2),
        name="relay",
    )(own, up, down)


UP = [(0, 1), (1, 2), (2, 3), (3, 0)]
DOWN = [(1, 0), (2, 1), (3, 2), (0, 3)]


def gather_source(block):
    n = lax.axis_size("panel")
    if n != 4:
        return gather_any(block)
    up = lax.ppermute(block, "panel", UP)
    down = lax.ppermute(block, "panel", DOWN)
    across = lax.ppermute(relay(block, up, down), "panel", [(0, 2), (3, 1), (2, 3), (1, 0)])
    return [block, up, down, across], (0, 3, 1, 2)


def gather_any(block):
    n = lax.axis_size("panel")
    return [
        block if d == 0 else lax.ppermute(block, "panel", [((i + d) % n, i) for i in range(n)])
        for d in range(n)
    ], tuple(range(n))


def gather_behind(block, k):
    n, zones = lax.axis_size("panel"), lax.axis_size("zone")
    if n != 4:
        return gather_any(lax.ppermute(block, "zone", [(i, (i + 1) % zones) for i in range(zones)]))
    both = ("panel", "zone")
    own = lax.ppermute(block, "zone", [(i, (i + 1) % zones) for i in range(zones)])
    across = lax.ppermute(
        block, both, [(p * zones + k - 1, (p + 2) % 4 * zones + k) for p in range(4)]
    )
    up, down = (
        lax.ppermute(own, both, [(p * zones + k, q * zones + k) for p, q in pairs])
        for pairs in (UP, DOWN)
    )
    return [own, across, up, down], (0, 2, 3, 1)


def product(ahead, n, matrix, blocks):
    me = lax.axis_index("panel")
    depth = blocks[0].shape[0]
    total = None
    for d, block in zip(ahead, blocks):
        start = pl.multiple_of(lax.rem(me + d, n) * depth, depth)
        part = jnp.dot(
            matrix[:, pl.ds(start, depth)], block[...], preferred_element_type=jnp.float32
        )
        total = part if total is None else total + part
    return total


def project_kernel(ahead, n, matrix, *refs):
    blocks, (wide, narrow) = refs[:n], refs[n:]
    total = product(ahead, n, matrix, blocks)
    wide[...] = total
    narrow[...] = total.astype(jnp.bfloat16)


def eliminate_kernel(ahead, n, k, matrix, wide, narrow, *refs):
    blocks, (out,) = refs[:n], refs[n:]
    total = product(ahead, n, matrix, blocks)
    mine = lax.axis_index("zone") == k
    out[...] = jnp.where(mine, (wide[...] - total).astype(jnp.bfloat16), narrow[...])


def project(matrix, blocks, ahead):
    n, (rows, _), cols = len(blocks), matrix.shape, blocks[0].shape[1]
    return pl.pallas_call(
        functools.partial(project_kernel, ahead, n),
        out_shape=(
            jax.ShapeDtypeStruct((rows, cols), jnp.float32),
            jax.ShapeDtypeStruct((rows, cols), jnp.bfloat16),
        ),
        in_specs=[VMEM] * (n + 1),
        out_specs=(VMEM,) * 2,
        compiler_params=params(8),
        name="project",
    )(matrix, *blocks)


def eliminate(matrix, blocks, ahead, wide, narrow, k):
    n, (rows, _), cols = len(blocks), matrix.shape, blocks[0].shape[1]
    return pl.pallas_call(
        functools.partial(eliminate_kernel, ahead, n, k),
        out_shape=jax.ShapeDtypeStruct((rows, cols), jnp.bfloat16),
        in_specs=[VMEM] * (n + 3),
        out_specs=VMEM,
        compiler_params=params(8),
        name="eliminate",
    )(matrix, wide, narrow, *blocks)


def local(source, inverse, coupling):
    inverse, coupling, source = inverse[0], coupling[0], source[0]
    zones = lax.axis_size("zone")
    width = source.shape[1] // CHUNKS
    inverse, coupling = fetch(inverse, coupling)
    results = []
    for c in range(CHUNKS):
        part = source[:, c * width : (c + 1) * width]
        wide, narrow = project(inverse, *gather_source(part))
        for k in range(1, zones):
            narrow = eliminate(coupling, *gather_behind(narrow, k), wide, narrow, k)
        results.append(narrow)
    return jnp.concatenate(results, 1)[None]


def solution(mesh):
    rows = P(("parts", "zone"), "panel", "rhs")
    square = P(("parts", "zone"), "panel", None)
    return jax.shard_map(
        local, mesh=mesh, in_specs=(rows, square, square), out_specs=rows, check_vma=False
    )
```

```python
import functools

import jax
import jax.numpy as jnp
from jax import lax
from jax.experimental import pallas as pl
from jax.experimental.pallas import tpu as pltpu
from jax.sharding import PartitionSpec as P

MIB = 1 << 20
VMEM = pl.BlockSpec(memory_space=pltpu.VMEM)
HBM = pl.BlockSpec(memory_space=pltpu.HBM)


def params(mib):
    return pltpu.CompilerParams(vmem_limit_bytes=mib * MIB)


def fetch_kernel(first, second, first_out, second_out, sems):
    copies = [
        pltpu.make_async_copy(first, first_out, sems.at[0]),
        pltpu.make_async_copy(second, second_out, sems.at[1]),
    ]
    for copy in copies:
        copy.start()
    for copy in copies:
        copy.wait()


def fetch(inverse, coupling):
    shape = jax.ShapeDtypeStruct(inverse.shape, inverse.dtype)
    return pl.pallas_call(
        fetch_kernel,
        out_shape=(shape, shape),
        in_specs=[HBM, HBM],
        out_specs=(VMEM, VMEM),
        scratch_shapes=[pltpu.SemaphoreType.DMA((2,))],
        compiler_params=params(18),
        name="fetch",
    )(inverse, coupling)


def relay_kernel(own, up, down, *rest):
    out = rest[-1]
    me = lax.axis_index("panel")

    @pl.when(me == 2)
    def _():
        out[...] = up[...]

    @pl.when(me == 1)
    def _():
        out[...] = down[...]

    @pl.when(jnp.logical_and(me != 1, me != 2))
    def _():
        out[...] = own[...]


def relay(own, up, down, after=()):
    return pl.pallas_call(
        relay_kernel,
        out_shape=jax.ShapeDtypeStruct(own.shape, own.dtype),
        in_specs=[VMEM] * 3 + [HBM] * len(after),
        out_specs=VMEM,
        compiler_params=params(2),
        name="relay",
    )(own, up, down, *after)


UP = [(0, 1), (1, 2), (2, 3), (3, 0)]
DOWN = [(1, 0), (2, 1), (3, 2), (0, 3)]
ACROSS = [(0, 2), (3, 1), (2, 3), (1, 0)]
STRAIGHT = [(p, (p + 2) % 4) for p in range(4)]
BOTH = ("panel", "zone")
together = lax.optimization_barrier


def to_next_zone(block):
    zones = lax.axis_size("zone")
    return lax.ppermute(block, "zone", [(i, (i + 1) % zones) for i in range(zones)])


def along_panel(block, pairs, source_zone, zone):
    zones = lax.axis_size("zone")
    return lax.ppermute(
        block, BOTH, [(p * zones + source_zone, q * zones + zone) for p, q in pairs]
    )


def product(ahead, matrix, blocks):
    me = lax.axis_index("panel")
    depth = blocks[0].shape[0]
    total = None
    for d, block in zip(ahead, blocks):
        start = pl.multiple_of(lax.rem(me + d, 4) * depth, depth)
        part = jnp.dot(
            matrix[:, pl.ds(start, depth)], block[...], preferred_element_type=jnp.float32
        )
        total = part if total is None else total + part
    return total


def begin_kernel(ahead, matrix, *refs):
    out = refs[-1]
    out[...] = product(ahead, matrix, refs[: len(ahead)])


def begin(matrix, blocks, ahead, after=()):
    (rows, _), cols = matrix.shape, blocks[0].shape[1]
    return pl.pallas_call(
        functools.partial(begin_kernel, ahead),
        out_shape=jax.ShapeDtypeStruct((rows, cols), jnp.float32),
        in_specs=[VMEM] * (len(blocks) + 1) + [HBM] * len(after),
        out_specs=VMEM,
        compiler_params=params(8),
        name="begin",
    )(matrix, *blocks, *after)


def project_kernel(matrix, begun, across, wide, narrow):
    total = begun[...] + product((2,), matrix, [across])
    wide[...] = total
    narrow[...] = total.astype(jnp.bfloat16)


def project(matrix, begun, across):
    return pl.pallas_call(
        project_kernel,
        out_shape=(
            jax.ShapeDtypeStruct(across.shape, jnp.float32),
            jax.ShapeDtypeStruct(across.shape, jnp.bfloat16),
        ),
        in_specs=[VMEM] * 3,
        out_specs=(VMEM,) * 2,
        compiler_params=params(8),
        name="project",
    )(matrix, begun, across)


def finish_kernel(k, matrix, *refs):
    halves, out = (refs[0:4], refs[4:8]), refs[8]
    mine = lax.axis_index("zone") == k
    cols = out.shape[1] // 2
    for half, (begun, across, wide, narrow) in enumerate(halves):
        total = begun[...] + product(((2,), (1,))[half], matrix, [across])
        left = (wide[...] - total).astype(jnp.bfloat16)
        out[:, half * cols : (half + 1) * cols] = jnp.where(mine, left, narrow[...])


def finish(matrix, first, second, k):
    rows, cols = first[-1].shape
    return pl.pallas_call(
        functools.partial(finish_kernel, k),
        out_shape=jax.ShapeDtypeStruct((rows, 2 * cols), jnp.bfloat16),
        in_specs=[VMEM] * 9,
        out_specs=VMEM,
        compiler_params=params(8),
        name="finish",
    )(matrix, *first, *second)


def local_four(source, inverse, coupling):
    zones = lax.axis_size("zone")
    width = source.shape[1] // 2
    first, second = source[:, :width], source[:, width:]
    inverse, coupling = fetch(inverse, coupling)

    up = lax.ppermute(first, "panel", UP)
    down = lax.ppermute(first, "panel", DOWN)
    up2 = lax.ppermute(second, "panel", UP)
    down2 = lax.ppermute(second, "panel", DOWN)
    passed = relay(first, up, down, (inverse, coupling))
    across = lax.ppermute(passed, "panel", ACROSS)
    begun = begin(inverse, [first, up, down], (0, 3, 1), (passed,))
    passed2 = relay(second, up2, down2)
    across2 = lax.ppermute(passed2, "panel", ACROSS)
    begun2 = begin(inverse, [second, up2, down2], (0, 3, 1), (passed2,))
    wide, narrow = project(inverse, begun, across)
    wide2, narrow2 = project(inverse, begun2, across2)

    for k in range(1, zones):
        own = to_next_zone(narrow)
        up = along_panel(own, UP, k, k)
        down = along_panel(own, DOWN, k, k)
        own2 = to_next_zone(narrow2)
        late, late2, own2 = together((narrow, narrow2, own2))
        across = along_panel(late, STRAIGHT, k - 1, k)
        across2 = along_panel(late2, STRAIGHT, k - 1, k)
        up2 = along_panel(own2, UP, k, k)
        down2 = along_panel(own2, DOWN, k, k)
        begun = begin(coupling, [own, up, down], (0, 3, 1))
        begun2 = begin(coupling, [own2, across2, up2], (0, 2, 3))
        both = finish(coupling, (begun, across, wide, narrow), (begun2, down2, wide2, narrow2), k)
        narrow, narrow2 = both[:, :width], both[:, width:]
    return both


def local_any(source, inverse, coupling):
    def gathered(block):
        return lax.all_gather(block, "panel", axis=0, tiled=True)

    wide = jnp.dot(inverse, gathered(source), preferred_element_type=jnp.float32)
    narrow = wide.astype(jnp.bfloat16)
    for k in range(1, lax.axis_size("zone")):
        behind = gathered(to_next_zone(narrow))
        left = wide - jnp.dot(coupling, behind, preferred_element_type=jnp.float32)
        narrow = jnp.where(lax.axis_index("zone") == k, left.astype(jnp.bfloat16), narrow)
    return narrow


def local(source, inverse, coupling):
    run = local_four if lax.axis_size("panel") == 4 else local_any
    return run(source[0], inverse[0], coupling[0])[None]


def solution(mesh):
    rows = P(("parts", "zone"), "panel", "rhs")
    square = P(("parts", "zone"), "panel", None)
    return jax.shard_map(
        local, mesh=mesh, in_specs=(rows, square, square), out_specs=rows, check_vma=False
    )
```

```python
import functools

import jax
import jax.numpy as jnp
from jax import lax
from jax.experimental import pallas as pl
from jax.experimental.pallas import tpu as pltpu
from jax.sharding import PartitionSpec as P

MIB = 1 << 20
VMEM = pl.BlockSpec(memory_space=pltpu.VMEM)
HBM = pl.BlockSpec(memory_space=pltpu.HBM)


def params(mib):
    return pltpu.CompilerParams(vmem_limit_bytes=mib * MIB)


def fetch_kernel(first, second, first_out, second_out, sems):
    copies = [
        pltpu.make_async_copy(first, first_out, sems.at[0]),
        pltpu.make_async_copy(second, second_out, sems.at[1]),
    ]
    for copy in copies:
        copy.start()
    for copy in copies:
        copy.wait()


def fetch(inverse, coupling):
    shape = jax.ShapeDtypeStruct(inverse.shape, inverse.dtype)
    return pl.pallas_call(
        fetch_kernel,
        out_shape=(shape, shape),
        in_specs=[HBM, HBM],
        out_specs=(VMEM, VMEM),
        scratch_shapes=[pltpu.SemaphoreType.DMA((2,))],
        compiler_params=params(18),
        name="fetch",
    )(inverse, coupling)


together = lax.optimization_barrier


def swap_panels(block, apart):
    return lax.ppermute(block, "panel", [(p, p ^ apart) for p in range(4)])


def across_zones(block, pairs):
    zones = lax.axis_size("zone")
    return lax.ppermute(
        block, ("panel", "zone"), [(a * zones + y, b * zones + z) for a, y, b, z in pairs]
    )


def swap_in_zone(block, apart, k):
    return across_zones(block, [(p, k, p ^ apart, k) for p in range(4)])


def swap_zones(block, k):
    return straight(block, 0, k)


def straight(block, apart, k):
    there = [(p, k - 1, p ^ apart, k) for p in range(4)]
    return across_zones(block, there + [(p, k, p, k - 1) for p in range(4)])


def product(apart, matrix, blocks):
    me = lax.axis_index("panel")
    depth = blocks[0].shape[0]
    total = None
    for d, block in zip(apart, blocks):
        start = pl.multiple_of((me ^ d) * depth, depth)
        part = jnp.dot(
            matrix[:, pl.ds(start, depth)], block[...], preferred_element_type=jnp.float32
        )
        total = part if total is None else total + part
    return total


def begin_kernel(apart, base, matrix, *refs):
    out = refs[-1]
    total = product(apart, matrix, refs[base : base + len(apart)])
    out[...] = refs[0][...] - total if base else total


def begin(matrix, blocks, apart, wide=None, after=()):
    (rows, _), cols = matrix.shape, blocks[0].shape[1]
    held = (matrix,) if wide is None else (matrix, wide)
    return pl.pallas_call(
        functools.partial(begin_kernel, apart, len(held) - 1),
        out_shape=jax.ShapeDtypeStruct((rows, cols), jnp.float32),
        in_specs=[VMEM] * (len(held) + len(blocks)) + [HBM] * len(after),
        out_specs=VMEM,
        compiler_params=params(8),
        name="begin",
    )(*held, *blocks, *after)


def project_kernel(matrix, begun, across, wide, narrow):
    total = begun[...] + product((2,), matrix, [across])
    wide[...] = total
    narrow[...] = total.astype(jnp.bfloat16)


def project(matrix, begun, across):
    return pl.pallas_call(
        project_kernel,
        out_shape=(
            jax.ShapeDtypeStruct(across.shape, jnp.float32),
            jax.ShapeDtypeStruct(across.shape, jnp.bfloat16),
        ),
        in_specs=[VMEM] * 3,
        out_specs=(VMEM,) * 2,
        compiler_params=params(8),
        name="project",
    )(matrix, begun, across)


def finish_kernel(plan, k, matrix, *refs):
    left, narrow, blocks, out = refs[0:2], refs[2:4], list(refs[4:-1]), refs[-1]
    me = lax.axis_index("panel")
    mine = lax.axis_index("zone") == k
    depth, cols = blocks[0].shape
    totals = [None, None]
    for apart, halves in plan:
        start = pl.multiple_of((me ^ apart) * depth, depth)
        here, blocks = [block[...] for block in blocks[: len(halves)]], blocks[len(halves) :]
        block = here[0] if len(here) == 1 else jnp.concatenate(here, axis=1)
        part = jnp.dot(
            matrix[:, pl.ds(start, depth)], block, preferred_element_type=jnp.float32
        )
        for i, half in enumerate(halves):
            mine_part = part[:, i * cols : (i + 1) * cols]
            totals[half] = mine_part if totals[half] is None else totals[half] + mine_part
    for half, total in enumerate(totals):
        rest = (left[half][...] - total).astype(jnp.bfloat16)
        out[:, half * cols : (half + 1) * cols] = jnp.where(mine, rest, narrow[half][...])


def finish(matrix, left, narrow, last, k):
    rows, cols = narrow[0].shape
    plan = tuple((apart, tuple(blocks)) for apart, blocks in last)
    operands = (matrix, *left, *narrow, *(b for _, blocks in last for b in blocks.values()))
    return pl.pallas_call(
        functools.partial(finish_kernel, plan, k),
        out_shape=jax.ShapeDtypeStruct((rows, 2 * cols), jnp.bfloat16),
        in_specs=[VMEM] * len(operands),
        out_specs=VMEM,
        compiler_params=params(8),
        name="finish",
    )(*operands)


def local_four(source, inverse, coupling):
    zones = lax.axis_size("zone")
    width = source.shape[1] // 2
    first, second = source[:, :width], source[:, width:]
    inverse, coupling = fetch(inverse, coupling)

    far = swap_panels(first, 3)
    near = swap_panels(first, 1)
    passed, _ = together((far, inverse))
    across = swap_panels(passed, 1)
    second, _ = together((second, far))
    far2 = swap_panels(second, 3)
    begun = begin(inverse, [first, near, far], (0, 1, 3))
    wide, narrow = project(inverse, begun, across)
    near2 = swap_panels(second, 1)
    across2 = swap_panels(far2, 1)
    begun2 = begin(inverse, [second, near2, far2], (0, 1, 3))
    wide2, narrow2 = project(inverse, begun2, across2)

    for k in range(1, zones):
        own = swap_zones(narrow, k)
        own2 = swap_zones(narrow2, k)
        far = swap_in_zone(own, 3, k)
        near = swap_in_zone(own, 1, k)
        across = swap_in_zone(far, 1, k)
        near2 = swap_in_zone(own2, 1, k)
        far2 = straight(narrow2, 3, k)
        across2 = straight(narrow2, 2, k)
        left = begin(coupling, [own, far, across], (0, 3, 2,), wide)
        left2 = begin(coupling, [own2, far2], (0, 3,), wide2)
        both = finish(
            coupling, (left, left2), (narrow, narrow2), [(1, {0: near, 1: near2}), (2, {1: across2})], k
        )
        narrow, narrow2 = both[:, :width], both[:, width:]
    return both


def local_any(source, inverse, coupling):
    def gathered(block):
        return lax.all_gather(block, "panel", axis=0, tiled=True)

    wide = jnp.dot(inverse, gathered(source), preferred_element_type=jnp.float32)
    narrow = wide.astype(jnp.bfloat16)
    zones = lax.axis_size("zone")
    for k in range(1, zones):
        sent = lax.ppermute(narrow, "zone", [(z, (z + 1) % zones) for z in range(zones)])
        behind = gathered(sent)
        left = wide - jnp.dot(coupling, behind, preferred_element_type=jnp.float32)
        narrow = jnp.where(lax.axis_index("zone") == k, left.astype(jnp.bfloat16), narrow)
    return narrow


def local(source, inverse, coupling):
    run = local_four if lax.axis_size("panel") == 4 else local_any
    return run(source[0], inverse[0], coupling[0])[None]


def solution(mesh):
    rows = P(("parts", "zone"), "panel", "rhs")
    square = P(("parts", "zone"), "panel", None)
    return jax.shard_map(
        local, mesh=mesh, in_specs=(rows, square, square), out_specs=rows, check_vma=False
    )
```

```python
import functools

import jax
import jax.numpy as jnp
from jax import lax
from jax.experimental import pallas as pl
from jax.experimental.pallas import tpu as pltpu
from jax.sharding import PartitionSpec as P

MIB = 1 << 20
VMEM = pl.BlockSpec(memory_space=pltpu.VMEM)
HBM = pl.BlockSpec(memory_space=pltpu.HBM)


def params(mib):
    return pltpu.CompilerParams(vmem_limit_bytes=mib * MIB)


def fetch_kernel(first, second, first_out, second_out, sems):
    copies = [
        pltpu.make_async_copy(first, first_out, sems.at[0]),
        pltpu.make_async_copy(second, second_out, sems.at[1]),
    ]
    for copy in copies:
        copy.start()
    for copy in copies:
        copy.wait()


def fetch(inverse, coupling):
    shape = jax.ShapeDtypeStruct(inverse.shape, inverse.dtype)
    return pl.pallas_call(
        fetch_kernel,
        out_shape=(shape, shape),
        in_specs=[HBM, HBM],
        out_specs=(VMEM, VMEM),
        scratch_shapes=[pltpu.SemaphoreType.DMA((2,))],
        compiler_params=params(18),
        name="fetch",
    )(inverse, coupling)


together = lax.optimization_barrier


def swap_panels(block, apart):
    return lax.ppermute(block, "panel", [(p, p ^ apart) for p in range(4)])


def across_zones(block, pairs):
    zones = lax.axis_size("zone")
    return lax.ppermute(
        block, ("panel", "zone"), [(a * zones + y, b * zones + z) for a, y, b, z in pairs]
    )


def swap_in_zone(block, apart, k):
    return across_zones(block, [(p, k, p ^ apart, k) for p in range(4)])


def swap_zones(block, k):
    return straight(block, 0, k)


def straight(block, apart, k):
    there = [(p, k - 1, p ^ apart, k) for p in range(4)]
    return across_zones(block, there + [(p, k, p, k - 1) for p in range(4)])


def product(apart, matrix, blocks):
    me = lax.axis_index("panel")
    depth = blocks[0].shape[0]
    total = None
    for d, block in zip(apart, blocks):
        start = pl.multiple_of((me ^ d) * depth, depth)
        part = jnp.dot(
            matrix[:, pl.ds(start, depth)], block[...], preferred_element_type=jnp.float32
        )
        total = part if total is None else total + part
    return total


def begin_kernel(apart, base, matrix, *refs):
    out = refs[-1]
    total = product(apart, matrix, refs[base : base + len(apart)])
    out[...] = refs[0][...] - total if base else total


def begin(matrix, blocks, apart, wide=None, after=()):
    (rows, _), cols = matrix.shape, blocks[0].shape[1]
    held = (matrix,) if wide is None else (matrix, wide)
    return pl.pallas_call(
        functools.partial(begin_kernel, apart, len(held) - 1),
        out_shape=jax.ShapeDtypeStruct((rows, cols), jnp.float32),
        in_specs=[VMEM] * (len(held) + len(blocks)) + [HBM] * len(after),
        out_specs=VMEM,
        compiler_params=params(8),
        name="begin",
    )(*held, *blocks, *after)


def project_kernel(matrix, begun, across, wide, narrow):
    total = begun[...] + product((2,), matrix, [across])
    wide[...] = total
    narrow[...] = total.astype(jnp.bfloat16)


def project(matrix, begun, across):
    return pl.pallas_call(
        project_kernel,
        out_shape=(
            jax.ShapeDtypeStruct(across.shape, jnp.float32),
            jax.ShapeDtypeStruct(across.shape, jnp.bfloat16),
        ),
        in_specs=[VMEM] * 3,
        out_specs=(VMEM,) * 2,
        compiler_params=params(8),
        name="project",
    )(matrix, begun, across)


def settle_kernel(k, matrix, left, left2, narrow, near, near2, first_out, left2_out):
    cols = near.shape[1]
    block = jnp.concatenate([near[...], near2[...]], axis=1)
    depth = block.shape[0]
    start = pl.multiple_of((lax.axis_index("panel") ^ 1) * depth, depth)
    part = jnp.dot(matrix[:, pl.ds(start, depth)], block, preferred_element_type=jnp.float32)
    rest = (left[...] - part[:, :cols]).astype(jnp.bfloat16)
    first_out[...] = jnp.where(lax.axis_index("zone") == k, rest, narrow[...])
    left2_out[...] = left2[...] - part[:, cols:]


def settle(matrix, left, left2, narrow, near, near2, k):
    return pl.pallas_call(
        functools.partial(settle_kernel, k),
        out_shape=(
            jax.ShapeDtypeStruct(narrow.shape, jnp.bfloat16),
            jax.ShapeDtypeStruct(left2.shape, jnp.float32),
        ),
        in_specs=[VMEM] * 6,
        out_specs=(VMEM,) * 2,
        compiler_params=params(8),
        name="settle",
    )(matrix, left, left2, narrow, near, near2)


def finish_kernel(apart, k, matrix, first, left2, narrow2, *refs):
    blocks, out = refs[:-1], refs[-1]
    cols = first.shape[1]
    rest = (left2[...] - product(apart, matrix, blocks)).astype(jnp.bfloat16)
    out[:, :cols] = first[...]
    out[:, cols:] = jnp.where(lax.axis_index("zone") == k, rest, narrow2[...])


def finish(matrix, first, left2, narrow2, blocks, apart, k):
    rows, cols = first.shape
    return pl.pallas_call(
        functools.partial(finish_kernel, apart, k),
        out_shape=jax.ShapeDtypeStruct((rows, 2 * cols), jnp.bfloat16),
        in_specs=[VMEM] * (4 + len(blocks)),
        out_specs=VMEM,
        compiler_params=params(8),
        name="finish",
    )(matrix, first, left2, narrow2, *blocks)


def local_four(source, inverse, coupling):
    zones = lax.axis_size("zone")
    width = source.shape[1] // 2
    first = source[:, :width]
    inverse, coupling = fetch(inverse, coupling)

    far = swap_panels(first, 3)
    near = swap_panels(first, 1)
    passed, _ = together((far, inverse))
    across = swap_panels(passed, 1)
    later, _ = together((source, inverse))
    second, _ = together((later[:, width:], far))
    far2 = swap_panels(second, 3)
    begun = begin(inverse, [first, near, far], (0, 1, 3))
    wide, narrow = project(inverse, begun, across)
    late, _ = together((second, across))
    near2 = swap_panels(late, 1)
    across2 = swap_panels(far2, 1)
    own = swap_zones(narrow, 1)
    begun2 = begin(inverse, [second, near2, far2], (0, 1, 3), after=(own,))
    wide2, narrow2 = project(inverse, begun2, across2)

    for k in range(1, zones):
        if k > 1:
            own = swap_zones(narrow, k)
        own2 = swap_zones(narrow2, k)
        far = swap_in_zone(own, 3, k)
        near = swap_in_zone(own, 1, k)
        across = swap_in_zone(far, 1, k)
        later, _ = together((narrow2, own2))
        far2 = swap_in_zone(own2, 3, k)
        near2 = straight(later, 1, k)
        across2 = straight(narrow2, 2, k)
        left = begin(coupling, [own, far, across], (0, 3, 2,), wide)
        left2 = begin(coupling, [own2, across2], (0, 2,), wide2)
        done, left2 = settle(coupling, left, left2, narrow, near, near2, k)
        both = finish(coupling, done, left2, narrow2, [far2], (3,), k)
        narrow, narrow2 = both[:, :width], both[:, width:]
    return both


def local_any(source, inverse, coupling):
    def gathered(block):
        return lax.all_gather(block, "panel", axis=0, tiled=True)

    wide = jnp.dot(inverse, gathered(source), preferred_element_type=jnp.float32)
    narrow = wide.astype(jnp.bfloat16)
    zones = lax.axis_size("zone")
    for k in range(1, zones):
        sent = lax.ppermute(narrow, "zone", [(z, (z + 1) % zones) for z in range(zones)])
        behind = gathered(sent)
        left = wide - jnp.dot(coupling, behind, preferred_element_type=jnp.float32)
        narrow = jnp.where(lax.axis_index("zone") == k, left.astype(jnp.bfloat16), narrow)
    return narrow


def local(source, inverse, coupling):
    run = local_four if lax.axis_size("panel") == 4 else local_any
    return run(source[0], inverse[0], coupling[0])[None]


def solution(mesh):
    rows = P(("parts", "zone"), "panel", "rhs")
    square = P(("parts", "zone"), "panel", None)
    return jax.shard_map(
        local, mesh=mesh, in_specs=(rows, square, square), out_specs=rows, check_vma=False
    )
```

```python
import functools

import jax
import jax.numpy as jnp
from jax import lax
from jax.experimental import pallas as pl
from jax.experimental.pallas import tpu as pltpu
from jax.sharding import PartitionSpec as P

MIB = 1 << 20
VMEM = pl.BlockSpec(memory_space=pltpu.VMEM)
HBM = pl.BlockSpec(memory_space=pltpu.HBM)


def params(mib):
    return pltpu.CompilerParams(vmem_limit_bytes=mib * MIB)


def fetch_kernel(first, second, first_out, second_out, sems):
    copies = [
        pltpu.make_async_copy(first, first_out, sems.at[0]),
        pltpu.make_async_copy(second, second_out, sems.at[1]),
    ]
    for copy in copies:
        copy.start()
    for copy in copies:
        copy.wait()


def fetch(inverse, coupling):
    shape = jax.ShapeDtypeStruct(inverse.shape, inverse.dtype)
    return pl.pallas_call(
        fetch_kernel,
        out_shape=(shape, shape),
        in_specs=[HBM, HBM],
        out_specs=(VMEM, VMEM),
        scratch_shapes=[pltpu.SemaphoreType.DMA((2,))],
        compiler_params=params(18),
        name="fetch",
    )(inverse, coupling)


together = lax.optimization_barrier


def swap_panels(block, apart):
    return lax.ppermute(block, "panel", [(p, p ^ apart) for p in range(4)])


def across_zones(block, pairs):
    zones = lax.axis_size("zone")
    return lax.ppermute(
        block, ("panel", "zone"), [(a * zones + y, b * zones + z) for a, y, b, z in pairs]
    )


def swap_in_zone(block, apart, k):
    return across_zones(block, [(p, k, p ^ apart, k) for p in range(4)])


def swap_zones(block, k):
    return straight(block, 0, k)


def straight(block, apart, k):
    there = [(p, k - 1, p ^ apart, k) for p in range(4)]
    return across_zones(block, there + [(p, k, p, k - 1) for p in range(4)])


def product(apart, matrix, blocks):
    me = lax.axis_index("panel")
    depth = blocks[0].shape[0]
    total = None
    for d, block in zip(apart, blocks):
        start = pl.multiple_of((me ^ d) * depth, depth)
        part = jnp.dot(
            matrix[:, pl.ds(start, depth)], block[...], preferred_element_type=jnp.float32
        )
        total = part if total is None else total + part
    return total


def begin_kernel(apart, base, matrix, *refs):
    out = refs[-1]
    total = product(apart, matrix, refs[base : base + len(apart)])
    out[...] = refs[0][...] - total if base else total


def begin(matrix, blocks, apart, wide=None, after=()):
    (rows, _), cols = matrix.shape, blocks[0].shape[1]
    held = (matrix,) if wide is None else (matrix, wide)
    return pl.pallas_call(
        functools.partial(begin_kernel, apart, len(held) - 1),
        out_shape=jax.ShapeDtypeStruct((rows, cols), jnp.float32),
        in_specs=[VMEM] * (len(held) + len(blocks)) + [HBM] * len(after),
        out_specs=VMEM,
        compiler_params=params(8),
        name="begin",
    )(*held, *blocks, *after)


def project_kernel(matrix, begun, across, wide, narrow):
    total = begun[...] + product((2,), matrix, [across])
    wide[...] = total
    narrow[...] = total.astype(jnp.bfloat16)


def project(matrix, begun, across):
    return pl.pallas_call(
        project_kernel,
        out_shape=(
            jax.ShapeDtypeStruct(across.shape, jnp.float32),
            jax.ShapeDtypeStruct(across.shape, jnp.bfloat16),
        ),
        in_specs=[VMEM] * 3,
        out_specs=(VMEM,) * 2,
        compiler_params=params(8),
        name="project",
    )(matrix, begun, across)


def settle_kernel(k, matrix, left, narrow, near, out):
    rest = (left[...] - product((1,), matrix, [near])).astype(jnp.bfloat16)
    out[...] = jnp.where(lax.axis_index("zone") == k, rest, narrow[...])


def settle(matrix, left, narrow, near, k):
    return pl.pallas_call(
        functools.partial(settle_kernel, k),
        out_shape=jax.ShapeDtypeStruct(narrow.shape, jnp.bfloat16),
        in_specs=[VMEM] * 4,
        out_specs=VMEM,
        compiler_params=params(8),
        name="settle",
    )(matrix, left, narrow, near)


def finish_kernel(apart, k, matrix, first, left2, narrow2, *refs):
    blocks, (out, rest, sems) = refs[:-3], refs[-3:]
    cols = first.shape[1]
    early = pltpu.make_async_copy(first, out.at[:, :cols], sems.at[0])
    early.start()
    total = (left2[...] - product(apart, matrix, blocks)).astype(jnp.bfloat16)
    rest[...] = jnp.where(lax.axis_index("zone") == k, total, narrow2[...])
    late = pltpu.make_async_copy(rest, out.at[:, cols:], sems.at[1])
    late.start()
    early.wait()
    late.wait()


def finish(matrix, first, left2, narrow2, blocks, apart, k):
    rows, cols = first.shape
    return pl.pallas_call(
        functools.partial(finish_kernel, apart, k),
        out_shape=jax.ShapeDtypeStruct((rows, 2 * cols), jnp.bfloat16),
        in_specs=[VMEM] * (4 + len(blocks)),
        out_specs=HBM,
        scratch_shapes=[pltpu.VMEM((rows, cols), jnp.bfloat16), pltpu.SemaphoreType.DMA((2,))],
        compiler_params=params(8),
        name="finish",
    )(matrix, first, left2, narrow2, *blocks)


def local_four(source, inverse, coupling):
    zones = lax.axis_size("zone")
    width = source.shape[1] // 2
    first = source[:, :width]
    inverse, coupling = fetch(inverse, coupling)

    far = swap_panels(first, 3)
    near = swap_panels(first, 1)
    passed, _ = together((far, inverse))
    across = swap_panels(passed, 1)
    later, _ = together((source, inverse))
    second, _ = together((later[:, width:], far))
    far2 = swap_panels(second, 3)
    begun = begin(inverse, [first, near, far], (0, 1, 3))
    wide, narrow = project(inverse, begun, across)
    late, _ = together((second, across))
    near2 = swap_panels(late, 1)
    across2 = swap_panels(far2, 1)
    own = swap_zones(narrow, 1)
    begun2 = begin(inverse, [second, near2, far2], (0, 1, 3), after=(own,))
    wide2, narrow2 = project(inverse, begun2, across2)

    for k in range(1, zones):
        if k > 1:
            own = swap_zones(narrow, k)
        own2 = swap_zones(narrow2, k)
        far = swap_in_zone(own, 3, k)
        near = swap_in_zone(own, 1, k)
        across = swap_in_zone(far, 1, k)
        later, _ = together((narrow2, own2))
        far2 = swap_in_zone(own2, 3, k)
        near2 = straight(later, 1, k)
        across2 = straight(later, 2, k)
        left = begin(coupling, [own, far, across], (0, 3, 2), wide)
        done = settle(coupling, left, narrow, near, k)
        left2 = begin(coupling, [own2], (0,), wide2)
        left2 = begin(coupling, [near2], (1,), left2)
        left2 = begin(coupling, [across2], (2,), left2)
        both = finish(coupling, done, left2, narrow2, [far2], (3,), k)
        narrow, narrow2 = both[:, :width], both[:, width:]
    return both


def local_any(source, inverse, coupling):
    def gathered(block):
        return lax.all_gather(block, "panel", axis=0, tiled=True)

    wide = jnp.dot(inverse, gathered(source), preferred_element_type=jnp.float32)
    narrow = wide.astype(jnp.bfloat16)
    zones = lax.axis_size("zone")
    for k in range(1, zones):
        sent = lax.ppermute(narrow, "zone", [(z, (z + 1) % zones) for z in range(zones)])
        behind = gathered(sent)
        left = wide - jnp.dot(coupling, behind, preferred_element_type=jnp.float32)
        narrow = jnp.where(lax.axis_index("zone") == k, left.astype(jnp.bfloat16), narrow)
    return narrow


def local(source, inverse, coupling):
    run = local_four if lax.axis_size("panel") == 4 else local_any
    return run(source[0], inverse[0], coupling[0])[None]


def solution(mesh):
    rows = P(("parts", "zone"), "panel", "rhs")
    square = P(("parts", "zone"), "panel", None)
    return jax.shard_map(
        local, mesh=mesh, in_specs=(rows, square, square), out_specs=rows, check_vma=False
    )
```

```python
import functools

import jax
import jax.numpy as jnp
from jax import lax
from jax.experimental import pallas as pl
from jax.experimental.pallas import tpu as pltpu
from jax.sharding import PartitionSpec as P

MIB = 1 << 20
VMEM = pl.BlockSpec(memory_space=pltpu.VMEM)
HBM = pl.BlockSpec(memory_space=pltpu.HBM)


def params(mib):
    return pltpu.CompilerParams(vmem_limit_bytes=mib * MIB)


def fetch_kernel(matrix, out, sem):
    copy = pltpu.make_async_copy(matrix, out, sem)
    copy.start()
    copy.wait()


def fetch(matrix):
    return pl.pallas_call(
        fetch_kernel,
        out_shape=jax.ShapeDtypeStruct(matrix.shape, matrix.dtype),
        in_specs=[HBM],
        out_specs=VMEM,
        scratch_shapes=[pltpu.SemaphoreType.DMA],
        compiler_params=params(10),
        name="fetch",
    )(matrix)


together = lax.optimization_barrier


def swap_panels(block, apart):
    return lax.ppermute(block, "panel", [(p, p ^ apart) for p in range(4)])


def across_zones(block, pairs):
    zones = lax.axis_size("zone")
    return lax.ppermute(
        block, ("panel", "zone"), [(a * zones + y, b * zones + z) for a, y, b, z in pairs]
    )


def swap_in_zone(block, apart, k):
    return across_zones(block, [(p, k, p ^ apart, k) for p in range(4)])


def swap_zones(block, k):
    return straight(block, 0, k)


def straight(block, apart, k):
    there = [(p, k - 1, p ^ apart, k) for p in range(4)]
    return across_zones(block, there + [(p, k, p, k - 1) for p in range(4)])


def product(apart, matrix, blocks):
    me = lax.axis_index("panel")
    depth = blocks[0].shape[0]
    total = None
    for d, block in zip(apart, blocks):
        start = pl.multiple_of((me ^ d) * depth, depth)
        part = jnp.dot(
            matrix[:, pl.ds(start, depth)], block[...], preferred_element_type=jnp.float32
        )
        total = part if total is None else total + part
    return total


def begin_kernel(apart, base, matrix, *refs):
    out = refs[-1]
    total = product(apart, matrix, refs[base : base + len(apart)])
    out[...] = refs[0][...] - total if base else total


def begin(matrix, blocks, apart, wide=None, after=()):
    (rows, _), cols = matrix.shape, blocks[0].shape[1]
    held = (matrix,) if wide is None else (matrix, wide)
    return pl.pallas_call(
        functools.partial(begin_kernel, apart, len(held) - 1),
        out_shape=jax.ShapeDtypeStruct((rows, cols), jnp.float32),
        in_specs=[VMEM] * (len(held) + len(blocks)) + [HBM] * len(after),
        out_specs=VMEM,
        compiler_params=params(8),
        name="begin",
    )(*held, *blocks, *after)


def project_kernel(matrix, begun, across, wide, narrow):
    total = begun[...] + product((2,), matrix, [across])
    wide[...] = total
    narrow[...] = total.astype(jnp.bfloat16)


def project(matrix, begun, across):
    return pl.pallas_call(
        project_kernel,
        out_shape=(
            jax.ShapeDtypeStruct(across.shape, jnp.float32),
            jax.ShapeDtypeStruct(across.shape, jnp.bfloat16),
        ),
        in_specs=[VMEM] * 3,
        out_specs=(VMEM,) * 2,
        compiler_params=params(8),
        name="project",
    )(matrix, begun, across)


def settle_kernel(k, matrix, left, narrow, near, out):
    rest = (left[...] - product((1,), matrix, [near])).astype(jnp.bfloat16)
    out[...] = jnp.where(lax.axis_index("zone") == k, rest, narrow[...])


def settle(matrix, left, narrow, near, k):
    return pl.pallas_call(
        functools.partial(settle_kernel, k),
        out_shape=jax.ShapeDtypeStruct(narrow.shape, jnp.bfloat16),
        in_specs=[VMEM] * 4,
        out_specs=VMEM,
        compiler_params=params(8),
        name="settle",
    )(matrix, left, narrow, near)


def finish_kernel(apart, k, matrix, first, left2, narrow2, *refs):
    blocks, (out, rest, sems) = refs[:-3], refs[-3:]
    cols = first.shape[1]
    early = pltpu.make_async_copy(first, out.at[:, :cols], sems.at[0])
    early.start()
    copies = [early]
    tall = first.shape[0] // 2
    for part in range(2):
        rows = slice(part * tall, (part + 1) * tall)
        total = (left2[rows] - product(apart, matrix.at[rows], blocks)).astype(jnp.bfloat16)
        rest[rows] = jnp.where(lax.axis_index("zone") == k, total, narrow2[rows])
        late = pltpu.make_async_copy(rest.at[rows], out.at[rows, cols:], sems.at[1 + part])
        late.start()
        copies.append(late)
    for copy in copies:
        copy.wait()


def finish(matrix, first, left2, narrow2, blocks, apart, k):
    rows, cols = first.shape
    return pl.pallas_call(
        functools.partial(finish_kernel, apart, k),
        out_shape=jax.ShapeDtypeStruct((rows, 2 * cols), jnp.bfloat16),
        in_specs=[VMEM] * (4 + len(blocks)),
        out_specs=HBM,
        scratch_shapes=[pltpu.VMEM((rows, cols), jnp.bfloat16), pltpu.SemaphoreType.DMA((3,))],
        compiler_params=params(8),
        name="finish",
    )(matrix, first, left2, narrow2, *blocks)


def local_four(source, inverse, coupling):
    zones = lax.axis_size("zone")
    width = source.shape[1] // 2
    first = source[:, :width]
    inverse, coupling = fetch(inverse), fetch(coupling)

    far = swap_panels(first, 3)
    near = swap_panels(first, 1)
    passed, _ = together((far, inverse))
    across = swap_panels(passed, 1)
    later, _ = together((source, inverse))
    second, _ = together((later[:, width:], far))
    far2 = swap_panels(second, 3)
    begun = begin(inverse, [first, near, far], (0, 1, 3), after=(coupling,))
    wide, narrow = project(inverse, begun, across)
    late, _ = together((second, across))
    near2 = swap_panels(late, 1)
    across2 = swap_panels(far2, 1)
    own = swap_zones(narrow, 1)
    begun2 = begin(inverse, [second, near2, far2], (0, 1, 3), after=(own,))
    wide2, narrow2 = project(inverse, begun2, across2)

    for k in range(1, zones):
        if k > 1:
            own = swap_zones(narrow, k)
        own2 = swap_zones(narrow2, k)
        far = swap_in_zone(own, 3, k)
        near = swap_in_zone(own, 1, k)
        across = swap_in_zone(far, 1, k)
        later, _ = together((narrow2, own2))
        far2 = swap_in_zone(own2, 3, k)
        near2 = straight(later, 1, k)
        across2 = straight(later, 2, k)
        left = begin(coupling, [own, far], (0, 3), wide)
        left = begin(coupling, [across], (2,), left)
        done = settle(coupling, left, narrow, near, k)
        left2 = begin(coupling, [own2], (0,), wide2)
        left2 = begin(coupling, [near2], (1,), left2)
        left2 = begin(coupling, [across2], (2,), left2)
        both = finish(coupling, done, left2, narrow2, [far2], (3,), k)
        narrow, narrow2 = both[:, :width], both[:, width:]
    return both


def local_any(source, inverse, coupling):
    def gathered(block):
        return lax.all_gather(block, "panel", axis=0, tiled=True)

    wide = jnp.dot(inverse, gathered(source), preferred_element_type=jnp.float32)
    narrow = wide.astype(jnp.bfloat16)
    zones = lax.axis_size("zone")
    for k in range(1, zones):
        sent = lax.ppermute(narrow, "zone", [(z, (z + 1) % zones) for z in range(zones)])
        behind = gathered(sent)
        left = wide - jnp.dot(coupling, behind, preferred_element_type=jnp.float32)
        narrow = jnp.where(lax.axis_index("zone") == k, left.astype(jnp.bfloat16), narrow)
    return narrow


def local(source, inverse, coupling):
    run = local_four if lax.axis_size("panel") == 4 else local_any
    return run(source[0], inverse[0], coupling[0])[None]


def solution(mesh):
    rows = P(("parts", "zone"), "panel", "rhs")
    square = P(("parts", "zone"), "panel", None)
    return jax.shard_map(
        local, mesh=mesh, in_specs=(rows, square, square), out_specs=rows, check_vma=False
    )
```

```python
import functools

import jax
import jax.numpy as jnp
from jax import lax
from jax.experimental import pallas as pl
from jax.experimental.pallas import tpu as pltpu
from jax.sharding import PartitionSpec as P

MIB = 1 << 20
VMEM = pl.BlockSpec(memory_space=pltpu.VMEM)
HBM = pl.BlockSpec(memory_space=pltpu.HBM)


def params(mib):
    return pltpu.CompilerParams(vmem_limit_bytes=mib * MIB)


def fetch_kernel(matrix, out, sem):
    copy = pltpu.make_async_copy(matrix, out, sem)
    copy.start()
    copy.wait()


def fetch(matrix):
    return pl.pallas_call(
        fetch_kernel,
        out_shape=jax.ShapeDtypeStruct(matrix.shape, matrix.dtype),
        in_specs=[HBM],
        out_specs=VMEM,
        scratch_shapes=[pltpu.SemaphoreType.DMA],
        compiler_params=params(10),
        name="fetch",
    )(matrix)


together = lax.optimization_barrier


def swap_panels(block, apart):
    return lax.ppermute(block, "panel", [(p, p ^ apart) for p in range(4)])


def across_zones(block, pairs):
    zones = lax.axis_size("zone")
    return lax.ppermute(
        block, ("panel", "zone"), [(a * zones + y, b * zones + z) for a, y, b, z in pairs]
    )


def swap_in_zone(block, apart, k):
    return across_zones(block, [(p, k, p ^ apart, k) for p in range(4)])


def swap_zones(block, k):
    return straight(block, 0, k)


def straight(block, apart, k):
    there = [(p, k - 1, p ^ apart, k) for p in range(4)]
    return across_zones(block, there + [(p, k, p, k - 1) for p in range(4)])


def product(apart, matrix, blocks):
    me = lax.axis_index("panel")
    depth = blocks[0].shape[0]
    total = None
    for d, block in zip(apart, blocks):
        start = pl.multiple_of((me ^ d) * depth, depth)
        part = jnp.dot(
            matrix[:, pl.ds(start, depth)], block[...], preferred_element_type=jnp.float32
        )
        total = part if total is None else total + part
    return total


def begin_kernel(apart, base, matrix, *refs):
    out = refs[-1]
    total = product(apart, matrix, refs[base : base + len(apart)])
    out[...] = refs[0][...] - total if base else total


def begin(matrix, blocks, apart, wide=None, after=()):
    (rows, _), cols = matrix.shape, blocks[0].shape[1]
    held = (matrix,) if wide is None else (matrix, wide)
    return pl.pallas_call(
        functools.partial(begin_kernel, apart, len(held) - 1),
        out_shape=jax.ShapeDtypeStruct((rows, cols), jnp.float32),
        in_specs=[VMEM] * (len(held) + len(blocks)) + [HBM] * len(after),
        out_specs=VMEM,
        compiler_params=params(8),
        name="begin",
    )(*held, *blocks, *after)


def project_kernel(matrix, begun, across, wide, narrow):
    total = begun[...] + product((2,), matrix, [across])
    wide[...] = total
    narrow[...] = total.astype(jnp.bfloat16)


def project(matrix, begun, across):
    return pl.pallas_call(
        project_kernel,
        out_shape=(
            jax.ShapeDtypeStruct(across.shape, jnp.float32),
            jax.ShapeDtypeStruct(across.shape, jnp.bfloat16),
        ),
        in_specs=[VMEM] * 3,
        out_specs=(VMEM,) * 2,
        compiler_params=params(8),
        name="project",
    )(matrix, begun, across)


def settle_kernel(k, matrix, left, narrow, near, out):
    rest = (left[...] - product((1,), matrix, [near])).astype(jnp.bfloat16)
    out[...] = jnp.where(lax.axis_index("zone") == k, rest, narrow[...])


def settle(matrix, left, narrow, near, k):
    return pl.pallas_call(
        functools.partial(settle_kernel, k),
        out_shape=jax.ShapeDtypeStruct(narrow.shape, jnp.bfloat16),
        in_specs=[VMEM] * 4,
        out_specs=VMEM,
        compiler_params=params(8),
        name="settle",
    )(matrix, left, narrow, near)


def finish_kernel(apart, k, matrix, first, left2, narrow2, *refs):
    blocks, (out, rest, sems) = refs[:-3], refs[-3:]
    cols = first.shape[1]
    early = pltpu.make_async_copy(first, out.at[:, :cols], sems.at[0])
    early.start()
    copies = [early]
    tall = first.shape[0] // 4
    for part in range(4):
        rows = slice(part * tall, (part + 1) * tall)
        total = (left2[rows] - product(apart, matrix.at[rows], blocks)).astype(jnp.bfloat16)
        rest[rows] = jnp.where(lax.axis_index("zone") == k, total, narrow2[rows])
        late = pltpu.make_async_copy(rest.at[rows], out.at[rows, cols:], sems.at[1 + part])
        late.start()
        copies.append(late)
    for copy in copies:
        copy.wait()


def finish(matrix, first, left2, narrow2, blocks, apart, k):
    rows, cols = first.shape
    return pl.pallas_call(
        functools.partial(finish_kernel, apart, k),
        out_shape=jax.ShapeDtypeStruct((rows, 2 * cols), jnp.bfloat16),
        in_specs=[VMEM] * (4 + len(blocks)),
        out_specs=HBM,
        scratch_shapes=[pltpu.VMEM((rows, cols), jnp.bfloat16), pltpu.SemaphoreType.DMA((5,))],
        compiler_params=params(8),
        name="finish",
    )(matrix, first, left2, narrow2, *blocks)


def local_four(source, inverse, coupling):
    zones = lax.axis_size("zone")
    width = source.shape[1] // 2
    first = source[:, :width]
    inverse, coupling = fetch(inverse), fetch(coupling)

    far = swap_panels(first, 3)
    near = swap_panels(first, 1)
    passed, _ = together((far, inverse))
    across = swap_panels(passed, 1)
    later, _ = together((source, inverse))
    second, _ = together((later[:, width:], far))
    far2 = swap_panels(second, 3)
    begun = begin(inverse, [first, near, far], (0, 1, 3), after=(coupling,))
    wide, narrow = project(inverse, begun, across)
    late, _ = together((second, across))
    near2 = swap_panels(late, 1)
    across2 = swap_panels(far2, 1)
    own = swap_zones(narrow, 1)
    begun2 = begin(inverse, [second, near2, far2], (0, 1, 3), after=(own,))
    wide2, narrow2 = project(inverse, begun2, across2)

    for k in range(1, zones):
        if k > 1:
            own = swap_zones(narrow, k)
        own2 = swap_zones(narrow2, k)
        far = swap_in_zone(own, 3, k)
        near = swap_in_zone(own, 1, k)
        across = swap_in_zone(far, 1, k)
        later, _ = together((narrow2, own2))
        far2 = swap_in_zone(own2, 3, k)
        near2 = straight(later, 1, k)
        across2 = straight(later, 2, k)
        left = begin(coupling, [own, far], (0, 3), wide)
        left = begin(coupling, [across], (2,), left)
        done = settle(coupling, left, narrow, near, k)
        left2 = begin(coupling, [own2], (0,), wide2)
        left2 = begin(coupling, [near2], (1,), left2)
        left2 = begin(coupling, [across2], (2,), left2)
        both = finish(coupling, done, left2, narrow2, [far2], (3,), k)
        narrow, narrow2 = both[:, :width], both[:, width:]
    return both


def local_any(source, inverse, coupling):
    def gathered(block):
        return lax.all_gather(block, "panel", axis=0, tiled=True)

    wide = jnp.dot(inverse, gathered(source), preferred_element_type=jnp.float32)
    narrow = wide.astype(jnp.bfloat16)
    zones = lax.axis_size("zone")
    for k in range(1, zones):
        sent = lax.ppermute(narrow, "zone", [(z, (z + 1) % zones) for z in range(zones)])
        behind = gathered(sent)
        left = wide - jnp.dot(coupling, behind, preferred_element_type=jnp.float32)
        narrow = jnp.where(lax.axis_index("zone") == k, left.astype(jnp.bfloat16), narrow)
    return narrow


def local(source, inverse, coupling):
    run = local_four if lax.axis_size("panel") == 4 else local_any
    return run(source[0], inverse[0], coupling[0])[None]


def solution(mesh):
    rows = P(("parts", "zone"), "panel", "rhs")
    square = P(("parts", "zone"), "panel", None)
    return jax.shard_map(
        local, mesh=mesh, in_specs=(rows, square, square), out_specs=rows, check_vma=False
    )
```
